32 devices in a mesh: groups: 2 (over x), row: 8 (over z, y), col: 2 (over core).
Axes of the slice: x: 2, y: 2, z: 4, core: 2. Of those that a mesh axis runs over, the one named last changes fastest.
Arguments:
- start_field: float32 [1024, 384, 256], P(('groups', 'row'), 'col'), parts along dimension 0, may hold values from 0 to 2
- counts: int32 [1024, 384, 256], P('groups', 'row', 'col'), parts along dimension 0, may hold values from -40 to 40
- weights: int32 [1024, 384, 256], P('groups', 'row', 'col'), parts along dimension 0, may hold values from 1 to 16
- strat_one: int32 [512, 512], replicated, may hold values from -64 to 63
- strat_two: int32 [384, 384], replicated, may hold values from -64 to 63
- strat_three: int32 [256, 256], replicated, may hold values from -64 to 63
Outputs:
- estimate: float32 [1024, 384, 256], P(('groups', 'row'), 'col'), parts along dimension 0
The draws below stay inside these ranges and needn't reach their ends.
There are 2 independent parts, one for each index of `groups`. The reference program is written for one: setup_inputs(seed, part) draws one part's arguments, and reference() takes and returns one part's arrays. A program takes and returns all parts, laid end to end along the dimension named above; an argument that names none is the same for every part. Nothing has to cross between parts.
All inputs are finite; a program needn't handle non-finite values.
Results may differ from the reference program's by a relative error of at most 0.0001.
Values sent between devices are 32-bit elements; how exact they have to be, the bound alone decides.
No kernel may reach another device: no remote copies, remote signals or barrier semaphores. Data moves between devices by JAX's collectives and lax.ppermute only.
A program may use at most 128 MiB of HBM per device.

```python
import math
import jax
import jax.numpy as jnp
from jax import lax

N1 = 512
N2 = 384
N3 = 256
STEPS = 1


def plant(values, rng, least, top_value):
    longest = values.shape.index(max(values.shape))
    spots = []
    for shift in (0, 1):
        where = [jax.random.randint(jax.random.fold_in(rng, axis), (), 0, length) for axis, length in enumerate(values.shape)]
        where[longest] = (where[longest] + shift) % values.shape[longest]
        spots.append(tuple(where))
    return values.at[spots[0]].set(least).at[spots[1]].set(top_value)


def shard_levels(rng, shape, split, smallest, high):
    level = 1.0
    for axis_at, blocks in split:
        heights = jax.random.uniform(jax.random.fold_in(jax.random.fold_in(rng, 6), axis_at), (blocks,), jnp.float32, smallest / len(split), high / len(split))
        level = level * jnp.repeat(jnp.exp(heights), shape[axis_at] // blocks).reshape((-1,) + (1,) * (len(shape) - 1 - axis_at))
    return level


def setup_inputs(seed: int = 0, part: int = 0) -> dict:
    arg_keys = jax.random.split(jax.random.key(seed), 7)
    part_splits = jax.random.split(jax.random.fold_in(arg_keys[6], part), 7)
    start_field = jnp.clip(2.0 * jax.random.uniform(part_splits[0], (N1, N2, N3), jnp.float32) ** shard_levels(part_splits[0], (N1, N2, N3), ((0, 8), (1, 2)), -0.2, 0.2), 0.0, 2.0)
    counts = plant(jax.random.randint(part_splits[1], (N1, N2, N3), -40, 41), jax.random.fold_in(part_splits[1], 1), -40, 40).astype(jnp.int32)
    weights = plant(jax.random.randint(part_splits[2], (N1, N2, N3), 1, 17), jax.random.fold_in(part_splits[2], 1), 1, 16).astype(jnp.int32)
    strat_one = plant(jax.random.randint(arg_keys[3], (N1, N1), -64, 64), jax.random.fold_in(arg_keys[3], 1), -64, 63).astype(jnp.int32)
    strat_two = plant(jax.random.randint(arg_keys[4], (N2, N2), -64, 64), jax.random.fold_in(arg_keys[4], 1), -64, 63).astype(jnp.int32)
    strat_three = plant(jax.random.randint(arg_keys[5], (N3, N3), -64, 64), jax.random.fold_in(arg_keys[5], 1), -64, 63).astype(jnp.int32)
    return {"start_field": start_field, "counts": counts, "weights": weights, "strat_one": strat_one, "strat_two": strat_two, "strat_three": strat_three}


highest = lax.Precision.HIGHEST
step_size = 0.5

def scaled(quant):
    order = quant.shape[0]
    return quant.astype(jnp.float32) * (1.0 / (37.0 * math.sqrt(order)))

def forward(field, first, second, third):
    field = jnp.einsum('ji,abi->abj', third, field, precision=highest)
    field = jnp.einsum('ji,aib->ajb', second, field, precision=highest)
    return jnp.einsum('ji,iab->jab', first, field, precision=highest)

def adjoint(field, first, second, third):
    field = jnp.einsum('ij,iab->jab', first, field, precision=highest)
    field = jnp.einsum('ij,aib->ajb', second, field, precision=highest)
    return jnp.einsum('ij,abi->abj', third, field, precision=highest)

def reference(start_field, counts, weights, strat_one, strat_two, strat_three):
    first = scaled(strat_one)
    second = scaled(strat_two)
    third = scaled(strat_three)
    weight_field = weights.astype(jnp.float32) / 16.0
    target = counts.astype(jnp.float32) / 16.0
    estimate = start_field
    for turn in range(STEPS):
        image = forward(estimate, first, second, third)
        residual = weight_field * (image - target)
        gradient = adjoint(residual, first, second, third)
        estimate = jnp.maximum(estimate - step_size * gradient, 0.0)
    return estimate
```

```python
import functools
import math

import jax
import jax.numpy as jnp
from jax import lax
from jax.experimental import pallas as pl
from jax.experimental.pallas import tpu as pltpu
from jax.sharding import PartitionSpec as P

highest = lax.Precision.HIGHEST
step_size = 0.5
f32 = jnp.float32
bf16 = jnp.bfloat16


def scale_of(order):
    return 1.0 / (37.0 * math.sqrt(order))


def scaled(quant):
    return quant.astype(f32) * scale_of(quant.shape[0])


def plain(start_field, counts, weights, strat_one, strat_two, strat_three):
    first, second, third = scaled(strat_one), scaled(strat_two), scaled(strat_three)
    field = jnp.einsum("ji,abi->abj", third, start_field, precision=highest)
    field = lax.all_to_all(field, "col", split_axis=2, concat_axis=1, tiled=True)
    field = jnp.einsum("ji,aib->ajb", second, field, precision=highest)
    field = lax.all_to_all(field, "row", split_axis=1, concat_axis=0, tiled=True)
    image = jnp.einsum("ji,iab->jab", first, field, precision=highest)
    field = weights.astype(f32) / 16.0 * (image - counts.astype(f32) / 16.0)
    field = jnp.einsum("ij,iab->jab", first, field, precision=highest)
    field = lax.all_to_all(field, "row", split_axis=0, concat_axis=1, tiled=True)
    field = jnp.einsum("ij,aib->ajb", second, field, precision=highest)
    field = lax.all_to_all(field, "col", split_axis=1, concat_axis=2, tiled=True)
    gradient = jnp.einsum("ij,abi->abj", third, field, precision=highest)
    return jnp.maximum(start_field - step_size * gradient, 0.0)


def halves(x):
    top = x.astype(bf16)
    return top, (x - top.astype(f32)).astype(bf16)


def mm(a, b):
    return jnp.dot(a, b, preferred_element_type=f32)


def third_kernel(x_ref, w_ref, own_ref, far_ref):
    ta, b, c = x_ref.shape
    hi, lo = halves(x_ref[...].reshape(ta * b, c))
    out = mm(jnp.concatenate([hi, lo], axis=1), w_ref[...])
    ch = own_ref.shape[2]
    own_ref[...] = out[:, :ch].reshape(ta, b, ch)
    far_ref[...] = out[:, ch:].reshape(ta, b, ch)


def second_kernel(own_ref, far_ref, w_ref, *outs):
    ta, _, c = own_ref.shape
    bh = outs[0].shape[1]
    for a in range(0, ta, 2):
        parts = []
        for ref in (own_ref, far_ref):
            parts += halves(jnp.concatenate([ref[a], ref[a + 1]], axis=1))
        out = mm(w_ref[...], jnp.concatenate(parts, axis=0))
        for m, o in enumerate(outs):
            o[a] = out[m * bh : (m + 1) * bh, :c]
            o[a + 1] = out[m * bh : (m + 1) * bh, c:]


def first_kernel(scale, n_in, n_out, *refs):
    pieces, (cnt_ref, wgt_ref, fwd_ref, bwd_ref) = refs[:n_in], refs[n_in : n_in + 4]
    outs = refs[n_in + 4 : n_in + 4 + n_out]
    rhs, res = refs[n_in + 4 + n_out :]
    n1, tb, c = cnt_ref.shape

    def flat(ref):
        return ref.reshape(ref.shape[0] * tb, c)

    def rows(ref, b):
        return flat(ref)[pl.ds(b, ref.shape[0], stride=tb), :]

    def step(p, carry):
        at = 0
        for ref in pieces:
            na = ref.shape[0]
            hi, lo = halves(jnp.concatenate([rows(ref, 2 * p), rows(ref, 2 * p + 1)], axis=1))
            rhs[at : at + na, :] = hi
            rhs[n1 + at : n1 + at + na, :] = lo
            at += na
        image = mm(fwd_ref[...], rhs[...])
        for j in range(2):
            wgt = rows(wgt_ref, 2 * p + j).astype(f32) * (1.0 / 16.0)
            tgt = rows(cnt_ref, 2 * p + j).astype(f32) * (1.0 / 16.0)
            hi, lo = halves(wgt * (image[:, j * c : (j + 1) * c] * scale - tgt))
            res[:n1, j * c : (j + 1) * c] = hi
            res[n1:, j * c : (j + 1) * c] = lo
        grad = mm(bwd_ref[...], res[...])
        at = 0
        for ref in outs:
            na = ref.shape[0]
            for j in range(2):
                flat(ref)[pl.ds(2 * p + j, na, stride=tb), :] = grad[at : at + na, j * c : (j + 1) * c]
            at += na
        return carry

    lax.fori_loop(0, tb // 2, step, 0)


def second_back_kernel(n_in, *refs):
    pieces, w_ref, own_ref, far_ref = refs[:n_in], refs[n_in], refs[n_in + 1], refs[n_in + 2]
    ta, bh, c = own_ref.shape
    for a in range(0, ta, 2):
        x = [jnp.concatenate([p[a], p[a + 1]], axis=1) for p in pieces]
        hi, lo = halves(jnp.concatenate(x, axis=0))
        out = mm(w_ref[...], jnp.concatenate([hi, lo], axis=0))
        for j in range(2):
            own_ref[a + j] = out[:bh, j * c : (j + 1) * c]
            far_ref[a + j] = out[bh:, j * c : (j + 1) * c]


def third_back_kernel(scale, x_ref, own_ref, far_ref, w_ref, *rest):
    out_ref = rest[-1]
    ta, b, c = x_ref.shape
    ch = own_ref.shape[2]
    oh, ol = halves(own_ref[...].reshape(ta * b, ch))
    fh, fl = halves(far_ref[...].reshape(ta * b, ch))
    grad = mm(jnp.concatenate([oh, fh, ol, fl], axis=1), w_ref[...])
    out_ref[...] = jnp.maximum(x_ref[...] - (grad * scale).reshape(ta, b, c), 0.0)


params = pltpu.CompilerParams(vmem_limit_bytes=60 * 2**20)


def cost(flops, nbytes):
    return pl.CostEstimate(flops=int(flops), bytes_accessed=int(nbytes), transcendentals=0)


def whole(array):
    return pl.BlockSpec(array.shape, lambda i: (0,) * array.ndim)


def tile_of(n, most):
    t = most
    while n % t:
        t //= 2
    return t


def pipelined(start_field, counts, weights, strat_one, strat_two, strat_three, rows, plan_f, plan_b, nh):
    al, bl, n3 = start_field.shape
    n1, bk, ch = counts.shape
    n2 = strat_two.shape[0]
    bh = bk // nh
    r, core = lax.axis_index("row"), lax.axis_index("col")
    scale = scale_of(n1) * scale_of(n2) * scale_of(n3)

    def own_first(a, axis):
        n = a.shape[axis] // 2
        return jnp.concatenate(
            [lax.dynamic_slice_in_dim(a, core * n, n, axis), lax.dynamic_slice_in_dim(a, (1 - core) * n, n, axis)], axis
        )

    def block(a, size, at, n, m, axis):
        return lax.dynamic_slice_in_dim(a, (r ^ m) * size + at, n, axis)

    third = own_first(strat_three.astype(bf16), 0)
    third_f = jnp.concatenate([third.T, third.T], axis=0)
    third_b = jnp.concatenate([third, third], axis=0)
    second = own_first(strat_two.astype(bf16), 1)
    second_h = [
        jnp.concatenate([block(second, bk, h * bh, bh, m, 0) for m in range(rows)], axis=0) for h in range(nh)
    ]
    second_f = [
        jnp.concatenate([s[:, :bl], s[:, :bl], s[:, bl:], s[:, bl:]], axis=1) for s in second_h
    ]
    second_t = jnp.concatenate(second_h, axis=0).T
    second_b = jnp.concatenate([second_t, second_t], axis=1)
    first = jnp.concatenate([block(strat_one.astype(bf16), al, 0, al, m, 1) for m in range(rows)], axis=1)
    first_f = jnp.concatenate([first, first], axis=1)
    first_b = jnp.concatenate([first.T, first.T], axis=1)

    swap = [(0, 1), (1, 0)]

    def trade(pieces):
        return [
            p if m == 0 else lax.ppermute(p, "row", [(i, i ^ m) for i in range(rows)]) for m, p in enumerate(pieces)
        ]

    chunks = sorted({(a0, na) for plan in plan_f for a0, na in plan if not any(
        (b0, nb) != (a0, na) and a0 <= b0 and b0 + nb <= a0 + na for p in plan_f for b0, nb in p)})
    y = {}
    for a0, na in chunks:
        ta = tile_of(math.gcd(na, a0) if a0 else na, 4)
        own, far = pl.pallas_call(
            third_kernel,
            grid=(na // ta,),
            in_specs=[pl.BlockSpec((ta, bl, n3), lambda i, o=a0 // ta: (i + o, 0, 0)), whole(third_f)],
            out_specs=[pl.BlockSpec((ta, bl, ch), lambda i: (i, 0, 0))] * 2,
            out_shape=[jax.ShapeDtypeStruct((na, bl, ch), f32)] * 2,
            compiler_params=params,
            cost_estimate=cost(4 * na * bl * n3 * n3, 8 * na * bl * n3),
            name="third",
        )(start_field, third_f)
        y[a0, na] = own, lax.ppermute(far, "col", swap)

    def second_part(h, a0, na):
        own, far = y[a0, na]
        ta = tile_of(na, 4)
        spec = pl.BlockSpec((ta, bl, ch), lambda i: (i, 0, 0))
        return trade(
            pl.pallas_call(
                second_kernel,
                grid=(na // ta,),
                in_specs=[spec, spec, whole(second_f[h])],
                out_specs=[pl.BlockSpec((ta, bh, ch), lambda i: (i, 0, 0))] * rows,
                out_shape=[jax.ShapeDtypeStruct((na, bh, ch), f32)] * rows,
                compiler_params=params,
                cost_estimate=cost(4 * na * bh * rows * n2 * ch, 4 * na * ch * (n2 + bh * rows)),
                name="second",
            )(own, far, second_f[h])
        )

    def first_part(h, got, plan):
        pieces = [got[k][m] for m in range(rows) for k in range(len(got))]
        shapes = [(na, bh, ch) for m in range(rows) for _, na in plan]
        spec = lambda s: pl.BlockSpec((s[0], 8, s[2]), lambda i: (0, i, 0))
        side = pl.BlockSpec((n1, 8, ch), lambda i, o=h * bh // 8: (0, i + o, 0))
        outs = pl.pallas_call(
            functools.partial(first_kernel, scale, len(pieces), len(shapes)),
            grid=(bh // 8,),
            in_specs=[spec(p.shape) for p in pieces] + [side, side, whole(first_f), whole(first_b)],
            out_specs=[spec(s) for s in shapes],
            out_shape=[jax.ShapeDtypeStruct(s, f32) for s in shapes],
            scratch_shapes=[pltpu.VMEM((2 * n1, 2 * ch), bf16)] * 2,
            compiler_params=params,
            cost_estimate=cost(8 * n1 * n1 * bh * ch, 16 * n1 * bh * ch),
            name="first",
        )(*pieces, counts, weights, first_f, first_b)
        k = len(plan)
        return [trade([outs[m * k + j] for m in range(rows)]) for j in range(k)]

    got_f = [[second_part(h, a0, na) for a0, na in plan_f[h]] for h in range(nh)]
    got_b = [first_part(h, got_f[h], plan_b[h]) for h in range(nh)]

    out = None
    for a0, na in plan_b[-1]:
        pieces, specs = [], []
        ta = tile_of(math.gcd(na, a0) if a0 else na, 4)
        for h in range(nh):
            (k, start) = next((k, s) for k, (s, n) in enumerate(plan_b[h]) if s <= a0 and a0 + na <= s + n)
            for m in range(rows):
                pieces.append(got_b[h][k][m])
                specs.append(pl.BlockSpec((ta, bh, ch), lambda i, o=(a0 - start) // ta: (i + o, 0, 0)))
        half = pl.BlockSpec((ta, bl, ch), lambda i: (i, 0, 0))
        own, far = pl.pallas_call(
            functools.partial(second_back_kernel, len(pieces)),
            grid=(na // ta,),
            in_specs=specs + [whole(second_b)],
            out_specs=[half] * 2,
            out_shape=[jax.ShapeDtypeStruct((na, bl, ch), f32)] * 2,
            compiler_params=params,
            cost_estimate=cost(4 * na * n2 * n2 * ch, 8 * na * n2 * ch),
            name="second_back",
        )(*pieces, second_b)
        far = lax.ppermute(far, "col", swap)
        full = pl.BlockSpec((ta, bl, n3), lambda i, o=a0 // ta: (i + o, 0, 0))
        extra = [] if out is None else [out]
        out = pl.pallas_call(
            functools.partial(third_back_kernel, step_size * scale),
            grid=(na // ta,),
            in_specs=[full, half, half, whole(third_b)] + [pl.BlockSpec(memory_space=pl.ANY)] * len(extra),
            out_specs=full,
            out_shape=jax.ShapeDtypeStruct(start_field.shape, f32),
            input_output_aliases={4: 0} if extra else {},
            compiler_params=params,
            cost_estimate=cost(4 * na * bl * n3 * n3, 12 * na * bl * n3),
            name="third_back",
        )(start_field, own, far, third_b, *extra)
    return out


def per_device(rows, cols, *args):
    start_field, counts = args[0], args[1]
    al, bl, n3 = start_field.shape
    n1, bk, ch = counts.shape
    nh = next((n for n in (2, 3, 1) if bk % (8 * n) == 0), 0)
    fits = cols == 2 and rows & (rows - 1) == 0 and 1 < rows <= 16 and nh and al % 64 == 0 and bl % 8 == 0 and ch % 128 == 0
    if not fits:
        return plain(*args)
    q = al // 4
    plan_f = [[(0, q), (q, al - q)]] * nh
    plan_b = [[(0, al)]] * (nh - 1) + [[(0, al - q), (al - q, q)]]
    return pipelined(*args, rows, plan_f, plan_b, nh)


def solution(mesh):
    placed = (
        P(("groups", "row"), "col", None),
        P("groups", "row", "col"),
        P("groups", "row", "col"),
        P(),
        P(),
        P(),
    )
    return jax.shard_map(
        functools.partial(per_device, mesh.shape["row"], mesh.shape["col"]),
        mesh=mesh,
        in_specs=placed,
        out_specs=P(("groups", "row"), "col", None),
        check_vma=False,
    )
```

```python
import functools
import math

import jax
import jax.numpy as jnp
from jax import lax
from jax.experimental import pallas as pl
from jax.experimental.pallas import tpu as pltpu
from jax.sharding import PartitionSpec as P


highest = lax.Precision.HIGHEST
step_size = 0.5
f32 = jnp.float32
bf16 = jnp.bfloat16


def scale_of(order):
    return 1.0 / (37.0 * math.sqrt(order))


def scaled(quant):
    return quant.astype(f32) * scale_of(quant.shape[0])


def plain(start_field, counts, weights, strat_one, strat_two, strat_three):
    first, second, third = scaled(strat_one), scaled(strat_two), scaled(strat_three)
    field = jnp.einsum("ji,abi->abj", third, start_field, precision=highest)
    field = lax.all_to_all(field, "col", split_axis=2, concat_axis=1, tiled=True)
    field = jnp.einsum("ji,aib->ajb", second, field, precision=highest)
    field = lax.all_to_all(field, "row", split_axis=1, concat_axis=0, tiled=True)
    image = jnp.einsum("ji,iab->jab", first, field, precision=highest)
    field = weights.astype(f32) / 16.0 * (image - counts.astype(f32) / 16.0)
    field = jnp.einsum("ij,iab->jab", first, field, precision=highest)
    field = lax.all_to_all(field, "row", split_axis=0, concat_axis=1, tiled=True)
    field = jnp.einsum("ij,aib->ajb", second, field, precision=highest)
    field = lax.all_to_all(field, "col", split_axis=1, concat_axis=2, tiled=True)
    gradient = jnp.einsum("ij,abi->abj", third, field, precision=highest)
    return jnp.maximum(start_field - step_size * gradient, 0.0)


def halves(x):
    top = x.astype(bf16)
    return top, (x - top.astype(f32)).astype(bf16)


def mm(a, b):
    return jnp.dot(a, b, preferred_element_type=f32)


def at_start(body):
    pl.when(pl.program_id(0) == 0)(body)


def span(start, size):
    return pl.ds(pl.multiple_of(start, 8), size)


def third_kernel(x_ref, a_ref, own_ref, far_ref, w):
    ta, b, c = x_ref.shape
    ch = own_ref.shape[2]
    core = lax.axis_index("col")

    @at_start
    def _():
        rows = jnp.concatenate([a_ref[span(core * ch, ch), :], a_ref[span((1 - core) * ch, ch), :]], axis=0)
        t = rows.astype(f32).T.astype(bf16)
        w[:c, :] = t
        w[c:, :] = t

    hi, lo = halves(x_ref[...].reshape(ta * b, c))
    out = mm(jnp.concatenate([hi, lo], axis=1), w[...])
    own_ref[...] = out[:, :ch].reshape(ta, b, ch)
    far_ref[...] = out[:, ch:].reshape(ta, b, ch)


def second_kernel(bk, start, own_ref, far_ref, a_ref, *refs):
    outs, (wf, w) = refs[:-2], refs[-2:]
    ta, bl, lanes = own_ref.shape
    n2 = 2 * bl
    bh = outs[0].shape[1]
    r, core = lax.axis_index("row"), lax.axis_index("col")

    @at_start
    def _():
        for m in range(len(outs)):
            wf[m * bh : (m + 1) * bh, :] = a_ref[span((r ^ m) * bk + start, bh), :].astype(f32)
        t = wf[...].astype(bf16)
        w[:, :n2] = t
        w[:, n2:] = t

    for a in range(0, ta, 2):
        own, far = (jnp.concatenate([ref[a], ref[a + 1]], axis=1) for ref in (own_ref, far_ref))
        parts = [halves(jnp.where(core == c, own, far)) for c in range(2)]
        out = mm(w[...], jnp.concatenate([p[i] for i in range(2) for p in parts], axis=0))
        for m, o in enumerate(outs):
            o[a] = out[m * bh : (m + 1) * bh, :lanes]
            o[a + 1] = out[m * bh : (m + 1) * bh, lanes:]


def first_kernel(scale, rows, k_in, k_out, k_old, *refs):
    n_in, n_out = rows * k_in, rows * k_out
    pieces, (cnt_ref, wgt_ref, fwd_ref, bwd_ref) = refs[:n_in], refs[n_in : n_in + 4]
    outs = refs[n_in + 4 + k_old : n_in + 4 + k_old + n_out]
    field, res = refs[n_in + 4 + k_old + n_out :]
    n1, tb, c = cnt_ref.shape
    al = n1 // rows
    r = lax.axis_index("row")

    def flat(ref):
        return ref.reshape(ref.shape[0] * tb, c)

    def lines(ref, b):
        return flat(ref)[pl.ds(b, ref.shape[0], stride=tb), :]

    def places(some, k):
        for m in range(rows):
            at = (r ^ m) * al
            for ref in some[m * k : (m + 1) * k]:
                yield ref, span(at, ref.shape[0])
                at = at + ref.shape[0]

    def step(p, carry):
        for ref, at in places(pieces, k_in):
            for j in range(2):
                field[at, j * c : (j + 1) * c] = lines(ref, 2 * p + j)
        image = mm(fwd_ref[...], jnp.concatenate(halves(field[...]), axis=0))
        for j in range(2):
            wgt = lines(wgt_ref, 2 * p + j).astype(f32) * (1.0 / 16.0)
            tgt = lines(cnt_ref, 2 * p + j).astype(f32) * (1.0 / 16.0)
            hi, lo = halves(wgt * (image[:, j * c : (j + 1) * c] * scale - tgt))
            res[:n1, j * c : (j + 1) * c] = hi
            res[n1:, j * c : (j + 1) * c] = lo
        field[...] = mm(bwd_ref[...], res[...])
        for ref, at in places(outs, k_out):
            for j in range(2):
                flat(ref)[pl.ds(2 * p + j, ref.shape[0], stride=tb), :] = field[at, j * c : (j + 1) * c]
        return carry

    lax.fori_loop(0, tb // 2, step, 0)


def second_back_kernel(bk, places, *refs):
    pieces, (w_ref, own_ref, far_ref, x) = refs[:-4], refs[-4:]
    ta, bl, c = own_ref.shape
    r = lax.axis_index("row")

    def step(k, carry):
        a = 2 * k
        for (m, b0), p in zip(places, pieces):
            x[span((r ^ m) * bk + b0, p.shape[1]), :] = jnp.concatenate([p[a], p[a + 1]], axis=1)
        hi, lo = halves(x[...])
        out = mm(w_ref[...], jnp.concatenate([hi, lo], axis=0))
        for j in range(2):
            own_ref[a + j] = out[:bl, j * c : (j + 1) * c]
            far_ref[a + j] = out[bl:, j * c : (j + 1) * c]
        return carry

    lax.fori_loop(0, ta // 2, step, 0)


def third_back_kernel(scale, x_ref, own_ref, far_ref, w_ref, *rest):
    out_ref = rest[-1]
    ta, b, c = x_ref.shape
    ch = own_ref.shape[2]
    oh, ol = halves(own_ref[...].reshape(ta * b, ch))
    fh, fl = halves(far_ref[...].reshape(ta * b, ch))
    grad = mm(jnp.concatenate([oh, fh, ol, fl], axis=1), w_ref[...])
    out_ref[...] = jnp.maximum(x_ref[...] - (grad * scale).reshape(ta, b, c), 0.0)


def params(mib):
    return pltpu.CompilerParams(vmem_limit_bytes=mib * 2**20)


def cost(flops, nbytes):
    return pl.CostEstimate(flops=int(flops), bytes_accessed=int(nbytes), transcendentals=0)


def whole(array):
    return pl.BlockSpec(array.shape, lambda i: (0,) * array.ndim)


def tile_of(n, most):
    t = most
    while n % t:
        t //= 2
    return t


def pipelined(start_field, counts, weights, strat_one, strat_two, strat_three, rows, chunks, plan_f, plan_b, ranges):
    al, bl, n3 = start_field.shape
    n1, bk, ch = counts.shape
    n2 = strat_two.shape[0]
    bh = bk // 2
    core = lax.axis_index("col")
    scale = scale_of(n1) * scale_of(n2) * scale_of(n3)
    swap = [(0, 1), (1, 0)]

    def trade(pieces):
        sent = [pieces[0]]
        for m in range(1, rows):
            sent.append(lax.ppermute(pieces[m], "row", [(i, i ^ m) for i in range(rows)]))
        return sent

    def trade_cores(piece):
        return lax.ppermute(piece, "col", swap)

    def step_of(a0, na):
        return tile_of(math.gcd(na, a0) if a0 else na, min(4, na // 4))

    def third_part(a0, na):
        ta = step_of(a0, na)
        own, far = pl.pallas_call(
            third_kernel,
            grid=(na // ta,),
            in_specs=[pl.BlockSpec((ta, bl, n3), lambda i: (i + a0 // ta, 0, 0)), whole(strat_three)],
            out_specs=[pl.BlockSpec((ta, bl, ch), lambda i: (i, 0, 0))] * 2,
            out_shape=[jax.ShapeDtypeStruct((na, bl, ch), f32)] * 2,
            scratch_shapes=[pltpu.VMEM((2 * n3, n3), bf16)],
            compiler_params=params(54),
            cost_estimate=cost(4 * na * bl * n3 * n3, 8 * na * bl * n3),
            name="third",
        )(start_field, strat_three)
        return own, trade_cores(far)

    def second_part(b0, nb, c):
        (_, na), (own, far) = chunks[c], y[c]
        ta = step_of(0, na)
        spec = pl.BlockSpec((ta, bl, ch), lambda i: (i, 0, 0))
        pieces = pl.pallas_call(
            functools.partial(second_kernel, bk, b0),
            grid=(na // ta,),
            in_specs=[spec, spec, whole(strat_two)],
            out_specs=[pl.BlockSpec((ta, nb, ch), lambda i: (i, 0, 0))] * rows,
            out_shape=[jax.ShapeDtypeStruct((na, nb, ch), f32)] * rows,
            scratch_shapes=[
                pltpu.VMEM((rows * nb, n2), f32),
                pltpu.VMEM((rows * nb, 2 * n2), bf16),
            ],
            compiler_params=params(48),
            cost_estimate=cost(4 * na * nb * rows * n2 * ch, 4 * na * ch * (n2 + nb * rows)),
            name="second",
        )(own, far, strat_two)
        return trade(pieces)

    y = [third_part(a0, na) for a0, na in chunks]
    got_f = [second_part(*part) for part in plan_f]

    late = lax.optimization_barrier((strat_one, strat_two, strat_three, got_f[0][0]))
    first = late[0].astype(bf16)
    first_f = jnp.concatenate([first, first], axis=1)
    first_b = jnp.concatenate([first.T, first.T], axis=1)

    def own_first(a, axis):
        n = a.shape[axis] // 2
        return jnp.concatenate(
            [lax.dynamic_slice_in_dim(a, core * n, n, axis), lax.dynamic_slice_in_dim(a, (1 - core) * n, n, axis)],
            axis,
        )

    second_t = own_first(late[1].astype(bf16), 1).T
    second_b = jnp.concatenate([second_t, second_t], axis=1)
    third = own_first(late[2].astype(bf16), 0)
    third_b = jnp.concatenate([third, third], axis=0)

    made = {}

    def first_part(h):
        pieces, specs = [], []
        for m in range(rows):
            for c, (_, na) in enumerate(chunks):
                (k, b0) = next((k, b) for k, (b, n, e) in enumerate(plan_f) if e == c and b <= h * bh < b + n)
                pieces.append(got_f[k][m])
                specs.append(pl.BlockSpec((na, 8, ch), lambda i, o=(h * bh - b0) // 8: (0, i + o, 0)))
        sets = sorted((a0, k) for k, (a0, _, b0, nb) in enumerate(plan_b) if b0 <= h * bh < b0 + nb)
        keys = [(k, m) for m in range(rows) for _, k in sets]
        old = [key for key in keys if key in made]
        out_specs, out_shape = [], []
        for k, _ in keys:
            _, na, b0, nb = plan_b[k]
            out_specs.append(pl.BlockSpec((na, 8, ch), lambda i, o=(h * bh - b0) // 8: (0, i + o, 0)))
            out_shape.append(jax.ShapeDtypeStruct((na, nb, ch), f32))
        side = pl.BlockSpec((n1, 8, ch), lambda i: (0, i + h * bh // 8, 0))
        outs = pl.pallas_call(
            functools.partial(first_kernel, scale, rows, len(chunks), len(sets), len(old)),
            grid=(bh // 8,),
            in_specs=specs
            + [side, side, whole(first_f), whole(first_b)]
            + [pl.BlockSpec(memory_space=pl.ANY)] * len(old),
            out_specs=out_specs,
            out_shape=out_shape,
            input_output_aliases={len(pieces) + 4 + i: keys.index(key) for i, key in enumerate(old)},
            scratch_shapes=[pltpu.VMEM((n1, 2 * ch), f32), pltpu.VMEM((2 * n1, 2 * ch), bf16)],
            compiler_params=params(60),
            cost_estimate=cost(8 * n1 * n1 * bh * ch, 16 * n1 * bh * ch),
            name="first",
        )(*pieces, counts, weights, first_f, first_b, *[made[key] for key in old])
        made.update(zip(keys, outs))

    first_part(0)
    first_part(1)
    got_b = [trade([made[k, m] for m in range(rows)]) for k in range(len(plan_b))]

    last = min(a0 for a0, na in ranges if na * bl * n3 <= 2**20)
    near = lax.slice_in_dim(start_field, last, al)

    out = None
    for a0, na in ranges:
        pieces, places, specs = [], [], []
        ta = step_of(a0, na)
        for k, (s0, n, b0, nb) in enumerate(plan_b):
            if s0 <= a0 and a0 + na <= s0 + n:
                for m in range(rows):
                    pieces.append(got_b[k][m])
                    places.append((m, b0))
                    specs.append(pl.BlockSpec((ta, nb, ch), lambda i, o=(a0 - s0) // ta: (i + o, 0, 0)))
        half = pl.BlockSpec((ta, bl, ch), lambda i: (i, 0, 0))
        own, far = pl.pallas_call(
            functools.partial(second_back_kernel, bk, places),
            grid=(na // ta,),
            in_specs=specs + [whole(second_b)],
            out_specs=[half] * 2,
            out_shape=[jax.ShapeDtypeStruct((na, bl, ch), f32)] * 2,
            scratch_shapes=[pltpu.VMEM((n2, 2 * ch), f32)],
            compiler_params=params(48),
            cost_estimate=cost(4 * na * n2 * n2 * ch, 8 * na * n2 * ch),
            name="second_back",
        )(*pieces, second_b)
        far = trade_cores(far)
        full = pl.BlockSpec((ta, bl, n3), lambda i, o=a0 // ta: (i + o, 0, 0))
        extra = [] if out is None else [out]
        x = start_field
        x_spec = full
        if a0 >= last:
            x_spec = pl.BlockSpec((ta, bl, n3), lambda i, o=(a0 - last) // ta: (i + o, 0, 0))
            x, own, far = (pltpu.with_memory_space_constraint(v, pltpu.VMEM) for v in (near, own, far))
        out = pl.pallas_call(
            functools.partial(third_back_kernel, step_size * scale),
            grid=(na // ta,),
            in_specs=[x_spec, half, half, whole(third_b)] + [pl.BlockSpec(memory_space=pl.ANY)] * len(extra),
            out_specs=full,
            out_shape=jax.ShapeDtypeStruct(start_field.shape, f32),
            input_output_aliases={4: 0} if extra else {},
            compiler_params=params(54),
            cost_estimate=cost(4 * na * bl * n3 * n3, 12 * na * bl * n3),
            name="third_back",
        )(x, own, far, third_b, *extra)
    return out


def plans(al, bk):
    e, bh = al // 8, bk // 2
    chunks = [(0, e), (e, 3 * e), (4 * e, 4 * e)]
    plan_f = [(0, bk, 0), (0, bh, 1), (0, bh, 2), (bh, bh, 1), (bh, bh, 2)]
    plan_b = [
        (0, 6 * e, 0, bh), (0, 3 * e, bh, bh), (3 * e, 3 * e, bh, bh), (6 * e, e, 0, bk), (7 * e, e, 0, bk),
    ]
    ranges = [(0, 3 * e), (3 * e, 3 * e), (6 * e, e), (7 * e, e)]
    return chunks, plan_f, plan_b, ranges


def per_device(rows, cols, *args):
    al, bl, _ = args[0].shape
    _, bk, ch = args[1].shape
    fits = cols == 2 and rows & (rows - 1) == 0 and 1 < rows <= 16 and al % 64 == 0 and bk % 16 == 0
    if not (fits and bl % 16 == 0 and ch % 128 == 0):
        return plain(*args)
    return pipelined(*args, rows, *plans(al, bk))


def solution(mesh):
    placed = (
        P(("groups", "row"), "col", None),
        P("groups", "row", "col"),
        P("groups", "row", "col"),
        P(),
        P(),
        P(),
    )
    return jax.shard_map(
        functools.partial(per_device, mesh.shape["row"], mesh.shape["col"]),
        mesh=mesh,
        in_specs=placed,
        out_specs=P(("groups", "row"), "col", None),
        check_vma=False,
    )
```
